512 devices in a mesh: dp: 64 (over x, z_lo, core), mp: 8 (over y, z_hi).
Axes of the slice: x: 4, y: 4, z: 16 (z_hi: 2, z_lo: 8; z = z_hi * 8 + z_lo), core: 2. Of those that a mesh axis runs over, the one named last changes fastest.
Arguments:
- master: float32 [8, 256, 512], P('mp', 'dp'), may hold values from -4 to 4
- moment: float32 [8, 256, 512], P('mp', 'dp'), may hold values from -0.06 to 0.06
- variance: float32 [8, 256, 512], P('mp', 'dp'), may hold values from 3e-06 to 3e-05
- flat_slot: int32 [256], replicated, may hold values from 0 to 255, each once
- feedback: bfloat16 [64, 2, 64, 8192], P('dp', None, 'mp'), may hold values from -0.029907227 to 0.029907227
- activations: bfloat16 [2, 8192, 8192], P(None, ('dp', 'mp')), may hold values from -24 to 24
- output_grads: bfloat16 [2, 8192, 8192], P(None, ('dp', 'mp')), may hold values from -24 to 24
Outputs:
- master_out: float32 [8, 256, 512], P('mp', 'dp')
- moment_out: float32 [8, 256, 512], P('mp', 'dp')
- feedback_out: bfloat16 [64, 2, 64, 8192], P('dp', None, 'mp')
The draws below stay inside these ranges and needn't reach their ends.
Inputs may be any that keep to these rules, and one draw needn't show every extreme that they name: `flat_slot`: every position of the flat buffer holds exactly one of the 256 segments.
All inputs are finite; a program needn't handle non-finite values. Where the reference program divides by a largest or mean magnitude, that divisor is 1e-20 or more.
Results may differ from the reference program's by a relative error of at most 0.0036.
The reference program's roundings to bfloat16 on the way (of `working` and `local_weights`) count: a program that leaves them out, or rounds other values in their place, can miss the bound.
Values may be sent and summed in bfloat16 or wider, within the bound.
A program may use at most 64 MiB of HBM per device.

```python
import math
import jax
import jax.numpy as jnp
from jax import lax

D = 8192
HID_DEV = 8
TOK = 128
SEG = 512
HID = 64
TOKENS = 8192
NSEG = 256
N_DP = 64
N_MP = 8


def spiked(array, stream_key, source, target, blocks, factor):
    owner, partner = [(jnp.arange(array.shape[position]) // (array.shape[position] // blocks)).reshape([-1 if axis == position else 1 for axis in range(array.ndim)]) for position in (source, target)]
    chosen = jax.random.permutation(stream_key, blocks)[partner]
    strong = (owner == chosen) | (owner == (partner + blocks // 2) % blocks)
    return jnp.where(strong, factor * array, array)


def block_levels(own_key, shape, cuts, smallest, largest):
    gain = 1.0
    for dim, shards_of in cuts:
        heights = jax.random.uniform(jax.random.fold_in(jax.random.fold_in(own_key, 6), dim), (shards_of,), jnp.float32, smallest / len(cuts), largest / len(cuts))
        gain = gain * jnp.repeat(jnp.exp(heights), shape[dim] // shards_of).reshape((-1,) + (1,) * (len(shape) - 1 - dim))
    return gain


def bell_draw(rng, dims, deviation, most, cuts=(), dtype=jnp.bfloat16):
    drawn = jax.random.normal(rng, dims, jnp.float32) * deviation
    if len(cuts) > 0:
        drawn = block_levels(rng, dims, cuts, -0.22, 0.18) * drawn
    return jnp.clip(drawn, min=-most, max=most).astype(dtype)


def bell_draw_with(own_key, shape, width, limit, cuts, heavy, dtype=jnp.bfloat16):
    entries = width * jax.random.normal(own_key, shape, jnp.float32)
    if cuts:
        entries = entries * block_levels(own_key, shape, cuts, -0.22, 0.18)
    return jnp.clip(spiked(entries, jax.random.fold_in(own_key, 3), *heavy), -limit, limit).astype(dtype)


def setup_inputs(seed: int = 0) -> dict:
    arg_keys = jax.random.split(jax.random.key(seed), 8)
    return {
        "master": bell_draw(arg_keys[0], (N_MP, NSEG, SEG), 1.0, 4.0, ((0, 8), (1, 64)), jnp.float32),
        "moment": bell_draw(arg_keys[1], (N_MP, NSEG, SEG), 0.01, 0.06, ((0, 8), (1, 64)), jnp.float32),
        "variance": jnp.clip(jnp.exp(math.log(2.9999999242136255e-05) - 2.30258503 * jax.random.uniform(arg_keys[2], (N_MP, NSEG, SEG), jnp.float32) ** block_levels(arg_keys[2], (N_MP, NSEG, SEG), ((0, 8), (1, 64)), -0.2, 0.2)), 3.000000106112566e-06, 2.9999999242136255e-05),
        "flat_slot": jax.random.permutation(arg_keys[3], NSEG).astype(jnp.int32),
        "feedback": bell_draw(arg_keys[4], (N_DP, 2, HID, D), 0.005, 0.029907227, ((0, 64), (2, 8))),
        "activations": bell_draw_with(arg_keys[5], (2, TOKENS, D), 1.0, 24.0, ((1, 512),), (1, 2, 512, 6.0)),
        "output_grads": bell_draw_with(arg_keys[6], (2, TOKENS, D), 1.0, 24.0, ((1, 512),), (1, 2, 512, 6.0)),
    }


beta_one = 0.9
step_rate = 0.05
epsilon = 1e-08
down_scale = 28672.0 ** (-0.5)

def tensor_order(flat, flat_slot):
    pieces = flat[:, flat_slot, :].reshape(N_MP, 2, HID_DEV, D)
    return jnp.transpose(pieces, (1, 0, 2, 3)).reshape(2, HID, D)

def flat_order(tensor, flat_slot):
    pieces = jnp.transpose(tensor.reshape(2, N_MP, HID_DEV, D), (1, 0, 2, 3)).reshape(N_MP, NSEG, SEG)
    return jnp.zeros_like(pieces).at[:, flat_slot, :].set(pieces)

def silu_slope(preact):
    sigmoid_value = jax.nn.sigmoid(preact)
    return sigmoid_value * (1.0 + preact * (1.0 - sigmoid_value))

def gradients(weights, inputs, cotangent):
    up_scale = D ** (-0.5)
    before = up_scale * jnp.dot(inputs, weights[0].T, preferred_element_type=jnp.float32)
    hidden = jax.nn.silu(before).astype(jnp.bfloat16)
    back_grad = down_scale * jnp.dot(cotangent, weights[1].T, preferred_element_type=jnp.float32)
    slope_grad = (back_grad * silu_slope(before)).astype(jnp.bfloat16)
    grad_up = up_scale * jnp.dot(slope_grad.T, inputs, preferred_element_type=jnp.float32)
    grad_down = down_scale * jnp.dot(hidden.T, cotangent, preferred_element_type=jnp.float32)
    return jnp.stack([grad_up, grad_down])

def reference(master, moment, variance, flat_slot, feedback, activations, output_grads):
    master_t = tensor_order(master, flat_slot)
    working = master_t.astype(jnp.bfloat16)
    moment_t = tensor_order(moment, flat_slot)
    denominator = jnp.sqrt(tensor_order(variance, flat_slot)) + epsilon
    inputs_all = activations.reshape(2, N_DP, TOK, D)
    grads_all = output_grads.reshape(2, N_DP, TOK, D)

    def worker(sums, things):
        first_inputs, second_inputs, first_grads, second_grads, residue = things
        step_one = gradients(working, first_inputs, first_grads)
        local_moment = beta_one * moment_t + (1.0 - beta_one) * step_one
        local_weights = (working.astype(jnp.float32) - step_rate * local_moment / denominator).astype(jnp.bfloat16)
        step_two = gradients(local_weights, second_inputs, second_grads)
        shifted = local_moment + residue.astype(jnp.float32)
        magnitude = lax.optimization_barrier(jnp.mean(jnp.abs(shifted), axis=-1, keepdims=True)) + 1e-06
        packed = magnitude * jnp.tanh(shifted / magnitude)
        new_error = (shifted - packed).astype(jnp.bfloat16)
        return ((sums[0] + packed, sums[1] + step_two), new_error)
    empty_sums = jnp.zeros((2, HID, D), jnp.float32)
    (moment_sum, grad_sum), feedback_out = lax.scan(worker, (empty_sums, empty_sums), (inputs_all[0], inputs_all[1], grads_all[0], grads_all[1], feedback))
    mean_moment = moment_sum / N_DP
    mean_grad = grad_sum / N_DP
    moment_new = beta_one * mean_moment + (1.0 - beta_one) * mean_grad
    master_new = master_t - step_rate * (mean_moment + moment_new) / denominator
    return (flat_order(master_new, flat_slot), flat_order(moment_new, flat_slot), feedback_out)
```

```python
import jax
import jax.numpy as jnp
from jax import lax
from jax.experimental import pallas as pl
from jax.experimental.pallas import tpu as pltpu
from jax.sharding import PartitionSpec as P

beta_one = 0.9
step_rate = 0.05
epsilon = 1e-08
down_scale = 28672.0 ** (-0.5)

D = 8192
HALF = D // 2
up_scale = D ** (-0.5)
SEG = 512
N_COPIES = 128
f32 = jnp.float32
bf16 = jnp.bfloat16


def silu_slope(preact):
    sigmoid_value = jax.nn.sigmoid(preact)
    return sigmoid_value * (1.0 + preact * (1.0 - sigmoid_value))


def one_hot(rows, index_row):
    positions = lax.broadcasted_iota(jnp.int32, (rows, index_row.shape[1]), 0)
    return jnp.where(positions == index_row, 1.0, 0.0).astype(bf16)


def dot_nt(a, b):
    return lax.dot_general(a, b, (((1,), (1,)), ((), ())), preferred_element_type=f32)


def dot_tn(a, b):
    return lax.dot_general(a, b, (((0,), (0,)), ((), ())), preferred_element_type=f32)


def dot_nn(a, b):
    return jnp.dot(a, b, preferred_element_type=f32)


def kernel(
    master, moment, variance, index, feedback, inputs, cotangents,
    master_out, moment_out, feedback_out,
    own, pay, zbuf, xs, gathered, weights, mom, den, mom_other, tok, partial, partial_in, grad_one,
    grad_send, grad_in, rows_p, flat_p, rc_p, sf_p, sb_p, rx_p, ff_p, fb_p, rz_p,
    rows_g, flat_g, rc_g, sf_g, sb_g, rx_g, ff_g, fb_g, rz_g,
    send_sem, recv_sem, local_sem,
):
    d, m = lax.axis_index("dp"), lax.axis_index("mp")
    x, zl, c = d // 16, (d % 16) // 2, d % 2
    y, zh = m // 2, m % 2
    z = zh * 8 + zl
    half = zh

    def at_z(to):
        return x * 16 + (to % 8) * 2 + c, y * 2 + to // 8

    def at_x(to):
        return to * 16 + zl * 2 + c, m

    def at_y(to):
        return d, to * 2 + zh

    core = (x * 16 + zl * 2 + (1 - c), m)
    partner = (d, y * 2 + (1 - zh))
    z_peers = [at_z((z + k) % 16) for k in range(1, 16)]
    zl_peers = [at_z(zh * 8 + (zl + k) % 8) for k in range(1, 8)]
    x_peers = [at_x((x + k) % 4) for k in range(1, 4)]
    y_peers = [at_y((y + k) % 4) for k in range(1, 4)]

    def place(peer):
        return {"dp": peer[0], "mp": peer[1]}

    barrier = pltpu.get_barrier_semaphore()
    for peer in z_peers + x_peers + y_peers + [core]:
        pl.semaphore_signal(
            barrier, inc=1, device_id=place(peer), device_id_type=pl.DeviceIdType.MESH
        )

    started = []

    def send(src, dst, peer):
        n = len(started)
        copy = pltpu.make_async_remote_copy(
            src_ref=src, dst_ref=dst, send_sem=send_sem.at[n], recv_sem=recv_sem.at[n],
            device_id=place(peer), device_id_type=pl.DeviceIdType.MESH,
        )
        copy.start()
        started.append(copy)
        return copy

    own[pl.ds(0, 4), :] = master[0].astype(bf16).astype(f32)
    high = moment[0].astype(bf16).astype(f32)
    own[pl.ds(4, 4), :] = high
    own[pl.ds(8, 4), :] = moment[0] - high
    own[pl.ds(12, 4), :] = variance[0]
    pay[...] = own[...].astype(bf16)
    zbuf[z] = own[...].astype(bf16)

    pl.semaphore_wait(barrier, 22)

    span_z = [send(pay, zbuf.at[z], peer) for peer in z_peers]

    sources = (inputs, cotangents)
    mine = pl.ds(pl.multiple_of(half * HALF, HALF), HALF)
    other = pl.ds(pl.multiple_of((1 - half) * HALF, HALF), HALF)
    block = pl.ds(pl.multiple_of(m * 16, 16), 16)
    block_partner = pl.ds(pl.multiple_of((y * 2 + 1 - zh) * 16, 16), 16)

    def tokens_z(s, a):
        return send(sources[a].at[s, :, other], tok.at[s, a, block, :], partner)

    def tokens_y(s, a):
        return [send(sources[a].at[s, :, mine], tok.at[s, a, block, :], p) for p in y_peers]

    def tokens_forward(s, a):
        held = tok.at[s, a, block_partner, :]
        return [send(held, held, p) for p in y_peers]

    across = {(0, a): tokens_z(0, a) for a in (0, 1)}
    arriving = {0: [], 1: []}
    for s in (0, 1):
        for a in (0, 1):
            arriving[s] += tokens_y(s, a)
    locals_ = []
    for s in (0, 1):
        for a in (0, 1):
            copy = pltpu.make_async_copy(
                sources[a].at[s, :, mine], tok.at[s, a, block, :], local_sem.at[2 * s + a]
            )
            copy.start()
            locals_.append(copy)
    across[(1, 0)] = tokens_z(1, 0)

    to = lax.broadcasted_iota(jnp.int32, (256, 256), 0)
    frm = lax.broadcasted_iota(jnp.int32, (256, 256), 1)
    wanted = ((to >> 2) & 15) * 16 + (to >> 6) * 4 + (to & 3)
    order = jnp.where(frm == wanted, 1.0, 0.0).astype(bf16)
    for copy in span_z:
        copy.wait_recv()
    ordered = dot_nn(order, zbuf[...].reshape(256, SEG)).astype(bf16)

    def span_rows(core_of, x_of):
        return pl.ds(pl.multiple_of((core_of * 4 + x_of) * 64, 64), 64)

    for kind in range(4):
        xs[kind] = ordered[kind * 64 : (kind + 1) * 64]
        gathered[kind, span_rows(c, x), :] = ordered[kind * 64 : (kind + 1) * 64]
    span_x = [send(xs, gathered.at[:, span_rows(c, x), :], p) for p in x_peers]
    span_core = [send(xs, gathered.at[:, span_rows(c, x), :], core)]
    for k in (1, 3, 2):
        span_x[k - 1].wait_recv()
        held = gathered.at[:, span_rows(c, (x + 4 - k) % 4), :]
        span_core.append(send(held, held, core))
    across[(0, 0)].wait_recv()
    arriving[0] += tokens_forward(0, 0)

    chosen = one_hot(512, index[pl.ds(half, 1), :])
    chosen_other = one_hot(512, index[pl.ds(4 + half, 1), :][:, :128])
    for copy in span_core:
        copy.wait_recv()
    across[(0, 1)].wait_recv()
    arriving[0] += tokens_forward(0, 1)

    spread = dot_tn(chosen, gathered[0])
    for cs in range(8):
        for p in range(2):
            lanes = slice(cs * SEG, (cs + 1) * SEG)
            weights[p, :, lanes] = spread[cs * 32 + p * 16 : cs * 32 + p * 16 + 16].astype(bf16)
    spread = dot_tn(chosen, gathered[1]) + dot_tn(chosen, gathered[2])
    for cs in range(8):
        for p in range(2):
            lanes = slice(cs * SEG, (cs + 1) * SEG)
            mom[p, :, lanes] = spread[cs * 32 + p * 16 : cs * 32 + p * 16 + 16]
    spread = jnp.sqrt(dot_tn(chosen, gathered[3])) + epsilon
    for cs in range(8):
        for p in range(2):
            lanes = slice(cs * SEG, (cs + 1) * SEG)
            den[p, :, lanes] = spread[cs * 32 + p * 16 : cs * 32 + p * 16 + 16]
    spread = dot_tn(chosen_other, gathered[1]) + dot_tn(chosen_other, gathered[2])
    for cs in range(8):
        mom_other[:, cs * SEG : (cs + 1) * SEG] = spread[cs * 16 : cs * 16 + 16]

    def products(s):
        partial[s, pl.ds(0, 16), :] = dot_nt(weights[0], tok[s, 0])
        partial[s, pl.ds(16, 16), :] = dot_nt(weights[1], tok[s, 1])
        return send(partial.at[s], partial_in.at[s], partner)

    def factors(s):
        before = up_scale * (partial[s, pl.ds(0, 16), :] + partial_in[s, pl.ds(0, 16), :])
        back = down_scale * (partial[s, pl.ds(16, 16), :] + partial_in[s, pl.ds(16, 16), :])
        hidden = (before * jax.nn.sigmoid(before)).astype(bf16)
        slope = (back * silu_slope(before)).astype(bf16)
        return slope, hidden

    for copy in arriving[0]:
        copy.wait_recv()
    locals_[0].wait()
    locals_[1].wait()
    exchange = products(0)
    across[(1, 1)] = tokens_z(1, 1)
    exchange.wait_recv()
    both = factors(0)
    for p in range(2):
        scale = (up_scale, down_scale)[p]
        for n in range(8):
            lanes = slice(n * SEG, (n + 1) * SEG)
            step_one = scale * dot_nn(both[p], tok[0, p, :, lanes])
            grad_one[p, :, lanes] = step_one
            local = beta_one * mom[p, :, lanes] + (1.0 - beta_one) * step_one
            mom[p, :, lanes] = local
            weights[p, :, lanes] = (
                weights[p, :, lanes].astype(f32) - step_rate * local / den[p, :, lanes]
            ).astype(bf16)
    own_rows = pl.ds(pl.multiple_of(zh * 8, 8), 8)
    partner_rows = pl.ds(pl.multiple_of((1 - zh) * 8, 8), 8)
    grad_send[...] = jnp.concatenate(
        [grad_one[0, partner_rows, :], grad_one[1, partner_rows, :]], axis=0
    ).astype(bf16)
    halves = send(grad_send, grad_in, partner)

    for a in (0, 1):
        across[(1, a)].wait_recv()
        arriving[1] += tokens_forward(1, a)
    for copy in arriving[1]:
        copy.wait_recv()
    locals_[2].wait()
    locals_[3].wait()
    exchange = products(1)

    halves.wait_recv()
    mom_other[...] = beta_one * mom_other[...] + (1.0 - beta_one) * grad_in[...].astype(f32)
    for p in range(2):
        mine_shifted = mom[p, own_rows, :] + feedback[0, p, :, mine].astype(f32)
        other_shifted = mom_other[pl.ds(p * 8, 8), :] + feedback[0, p, :, other].astype(f32)
        total = jnp.sum(jnp.abs(mine_shifted), axis=-1, keepdims=True) + jnp.sum(
            jnp.abs(other_shifted), axis=-1, keepdims=True
        )
        magnitude = total / D + 1e-06
        for which, shifted, lanes in ((half, mine_shifted, mine), (1 - half, other_shifted, other)):
            packed = magnitude * jnp.tanh(shifted / magnitude)
            feedback_out[0, p, :, lanes] = (shifted - packed).astype(bf16)
            for cs in range(8):
                row = pl.multiple_of((which * 8 + cs) * 16 + p * 8, 8)
                rows_p[pl.ds(row, 8), :] = packed[:, cs * SEG : (cs + 1) * SEG]
    chosen_p = one_hot(256, index[pl.ds(2, 1), :])
    flat_p[...] = dot_nn(chosen_p, rows_p[...].astype(bf16)).astype(bf16)

    def reduce_core(flat, rc, nz):
        rows = 16 * nz
        return send(flat.at[pl.ds(pl.multiple_of((1 - c) * rows, rows), rows), :], rc, core)

    def reduce_x(copy, flat, rc, sf, sb, rx, nz):
        rows, part = 16 * nz, 4 * nz
        copy.wait_recv()
        total = flat[pl.ds(pl.multiple_of(c * rows, rows), rows), :].astype(f32) + rc[...].astype(f32)
        sf[...] = total
        sb[...] = total.astype(bf16)
        return [
            send(sb.at[pl.ds(pl.multiple_of(((x + k) % 4) * part, part), part), :], rx.at[k - 1], x_peers[k - 1])
            for k in range(1, 4)
        ]

    def reduce_z(copies, sf, rx, ff, fb, rz, nz, peers, me):
        part = 4 * nz
        for copy in copies:
            copy.wait_recv()
        total = sf[pl.ds(pl.multiple_of(x * part, part), part), :]
        for k in range(3):
            total = total + rx[k].astype(f32)
        for i in range(nz):
            for t in range(4):
                ff[i, pl.ds(t * 4, 4), :] = total[i * 4 : i * 4 + 4, t * 128 : (t + 1) * 128]
        fb[...] = ff[...].astype(bf16)
        return [
            send(fb.at[(me + k) % nz], rz.at[k - 1], peers[k - 1]) for k in range(1, nz)
        ]

    def reduce_end(copies, ff, rz, nz, me):
        for copy in copies:
            copy.wait_recv()
        total = ff[me]
        for k in range(nz - 1):
            total = total + rz[k].astype(f32)
        return jnp.concatenate([total[t * 4 : t * 4 + 4] for t in range(4)], axis=1)

    step_p = reduce_core(flat_p, rc_p, 8)
    exchange.wait_recv()
    both = factors(1)
    for p in range(2):
        scale = (up_scale, down_scale)[p]
        for n in range(8):
            step_two = scale * dot_nn(both[p], tok[1, p, :, n * SEG : (n + 1) * SEG])
            rows_g[pl.ds(n * 32 + p * 16, 16), :] = step_two.astype(bf16)
    flat_g[...] = dot_nn(chosen, rows_g[...]).astype(bf16)
    step_g = reduce_core(flat_g, rc_g, 16)
    step_p = reduce_x(step_p, flat_p, rc_p, sf_p, sb_p, rx_p, 8)
    step_g = reduce_x(step_g, flat_g, rc_g, sf_g, sb_g, rx_g, 16)
    step_p = reduce_z(step_p, sf_p, rx_p, ff_p, fb_p, rz_p, 8, zl_peers, zl)
    step_g = reduce_z(step_g, sf_g, rx_g, ff_g, fb_g, rz_g, 16, z_peers, z)
    mean_moment = reduce_end(step_p, ff_p, rz_p, 8, zl) / 64
    mean_grad = reduce_end(step_g, ff_g, rz_g, 16, z) / 64
    moment_new = beta_one * mean_moment + (1.0 - beta_one) * mean_grad
    moment_out[0] = moment_new
    owner_denominator = jnp.sqrt(variance[0]) + epsilon
    master_out[0] = master[0] - step_rate * (mean_moment + moment_new) / owner_denominator
    for copy in started:
        copy.wait_send()


def index_table(flat_slot):
    slot = jnp.transpose(flat_slot.reshape(2, 8, 16), (2, 0, 1))
    owner, within = slot // 4, slot % 4
    lane = (owner % 2) * 4 + owner // 16
    low = (owner % 16) // 2
    span = lane * 64 + low * 4 + within
    both = jnp.stack([span, span + 32], axis=2).reshape(2, 256)
    packed = (lane * 32 + low * 4 + within).reshape(1, 256)
    other = jnp.stack([span[8:].reshape(128), span[:8].reshape(128) + 32])
    other = jnp.pad(other, ((0, 0), (0, 128)))
    blank = jnp.zeros((1, 256), jnp.int32)
    return jnp.concatenate([both, packed, blank, other, blank, blank], axis=0)


def per_device(master, moment, variance, flat_slot, feedback, activations, output_grads):
    vmem = pl.BlockSpec(memory_space=pltpu.VMEM)
    hbm = pl.BlockSpec(memory_space=pl.ANY)

    def reduction(nz):
        return [
            pltpu.VMEM((32 * nz, SEG), bf16),
            pltpu.VMEM((16 * nz, SEG), bf16),
            pltpu.VMEM((16 * nz, SEG), f32),
            pltpu.VMEM((16 * nz, SEG), bf16),
            pltpu.VMEM((3, 4 * nz, SEG), bf16),
            pltpu.VMEM((nz, 16, 128), f32),
            pltpu.VMEM((nz, 16, 128), bf16),
            pltpu.VMEM((nz - 1, 16, 128), bf16),
        ]

    scratch = [
        pltpu.VMEM((16, SEG), f32),
        pltpu.VMEM((16, SEG), bf16),
        pltpu.VMEM((16, 16, SEG), bf16),
        pltpu.VMEM((4, 64, SEG), bf16),
        pltpu.VMEM((4, 512, SEG), bf16),
        pltpu.VMEM((2, 16, HALF), bf16),
        pltpu.VMEM((2, 16, HALF), f32),
        pltpu.VMEM((2, 16, HALF), f32),
        pltpu.VMEM((16, HALF), f32),
        pltpu.VMEM((2, 2, 128, HALF), bf16),
        pltpu.VMEM((2, 32, 128), f32),
        pltpu.VMEM((2, 32, 128), f32),
        pltpu.VMEM((2, 16, HALF), f32),
        pltpu.VMEM((16, HALF), bf16),
        pltpu.VMEM((16, HALF), bf16),
        pltpu.VMEM((256, SEG), f32),
        *reduction(8),
        pltpu.VMEM((256, SEG), bf16),
        *reduction(16),
        pltpu.SemaphoreType.DMA((N_COPIES,)),
        pltpu.SemaphoreType.DMA((N_COPIES,)),
        pltpu.SemaphoreType.DMA((4,)),
    ]
    return pl.pallas_call(
        kernel,
        out_shape=(
            jax.ShapeDtypeStruct(master.shape, f32),
            jax.ShapeDtypeStruct(moment.shape, f32),
            jax.ShapeDtypeStruct(feedback.shape, bf16),
        ),
        in_specs=[vmem] * 5 + [hbm] * 2,
        out_specs=(vmem,) * 3,
        scratch_shapes=scratch,
        compiler_params=pltpu.CompilerParams(collective_id=0, has_side_effects=True),
        name="window",
    )(master, moment, variance, index_table(flat_slot), feedback, activations, output_grads)


def solution(mesh):
    in_specs = (
        P("mp", "dp", None),
        P("mp", "dp", None),
        P("mp", "dp", None),
        P(),
        P("dp", None, "mp", None),
        P(None, ("dp", "mp"), None),
        P(None, ("dp", "mp"), None),
    )
    out_specs = (P("mp", "dp", None), P("mp", "dp", None), P("dp", None, "mp", None))
    return jax.shard_map(
        per_device, mesh=mesh, in_specs=in_specs, out_specs=out_specs, check_vma=False
    )
```

```python
import jax
import jax.numpy as jnp
from jax import lax
from jax.experimental import pallas as pl
from jax.experimental.pallas import tpu as pltpu
from jax.sharding import PartitionSpec as P

beta_one = 0.9
step_rate = 0.05
epsilon = 1e-08
down_scale = 28672.0 ** (-0.5)

D = 8192
QUARTER = D // 4
up_scale = D ** (-0.5)
SEG = 512
N_COPIES = 160
f32 = jnp.float32
bf16 = jnp.bfloat16


def silu_slope(preact):
    sigmoid_value = jax.nn.sigmoid(preact)
    return sigmoid_value * (1.0 + preact * (1.0 - sigmoid_value))


def dot_nt(a, b):
    return lax.dot_general(a, b, (((1,), (1,)), ((), ())), preferred_element_type=f32)


def dot_tn(a, b):
    return lax.dot_general(a, b, (((0,), (0,)), ((), ())), preferred_element_type=f32)


def dot_nn(a, b):
    return jnp.dot(a, b, preferred_element_type=f32)


def kernel(
    master_hbm, moment_hbm, variance_hbm, slot_hbm, feedback_hbm, inputs, cotangents,
    master_out, moment_out, feedback_out,
    master, moment, variance, slot, feedback, own, pay, zbuf, xs, gathered, chosen, weights, mom, den,
    tok_one, tok_two,
    rows_p, flat_p, rc_p, sf_p, sb_p, rx_p, ff_p, fb_p, rz_p,
    rows_g, flat_g, rc_g, sf_g, sb_g, rx_g, ff_g, fb_g, rz_g,
    send_sem, recv_sem, local_sem,
):
    d, m = lax.axis_index("dp"), lax.axis_index("mp")
    x, zl, c = d // 16, (d % 16) // 2, d % 2
    y, zh = m // 2, m % 2
    z = zh * 8 + zl

    def at_z(to):
        return x * 16 + (to % 8) * 2 + c, y * 2 + to // 8

    def at_x(to):
        return to * 16 + zl * 2 + c, m

    def at_y(to):
        return d, to * 2 + zh

    core = (x * 16 + zl * 2 + (1 - c), m)
    z_peers = [at_z((z + k) % 16) for k in range(1, 16)]
    partner = z_peers[7]
    zl_peers = [at_z(zh * 8 + (zl + k) % 8) for k in range(1, 8)]
    x_peers = [at_x((x + k) % 4) for k in range(1, 4)]
    y_peers = [at_y((y + k) % 4) for k in range(1, 4)]

    def place(peer):
        return {"dp": peer[0], "mp": peer[1]}

    barrier = pltpu.get_barrier_semaphore()
    for peer in z_peers + x_peers + y_peers + [core]:
        pl.semaphore_signal(
            barrier, inc=1, device_id=place(peer), device_id_type=pl.DeviceIdType.MESH
        )

    started, held_here = [], []

    def send(src, dst, peer):
        n = len(started)
        copy = pltpu.make_async_remote_copy(
            src_ref=src, dst_ref=dst, send_sem=send_sem.at[n], recv_sem=recv_sem.at[n],
            device_id=place(peer), device_id_type=pl.DeviceIdType.MESH,
        )
        copy.start()
        started.append(copy)
        return copy

    def local(src, dst):
        copy = pltpu.make_async_copy(src, dst, local_sem.at[len(held_here)])
        copy.start()
        held_here.append(copy)
        return copy

    sources = (inputs, cotangents)
    rows_one = pl.ds(pl.multiple_of(m * 16, 16), 16)
    rows_partner = pl.ds(pl.multiple_of((y * 2 + 1 - zh) * 16, 16), 16)
    rows_two = pl.ds(pl.multiple_of(y * 16, 16), 16)
    small = [
        local(master_hbm, master), local(moment_hbm, moment), local(variance_hbm, variance),
    ]
    later = [local(slot_hbm, slot), local(feedback_hbm, feedback)]
    for a in (0, 1):
        later.append(local(sources[a].at[0], tok_one.at[a, rows_one, :]))
        later.append(local(sources[a].at[1], tok_two.at[a, rows_two, :]))
    for copy in small:
        copy.wait()

    own[pl.ds(0, 4), :] = master[0].astype(bf16).astype(f32)
    high = moment[0].astype(bf16).astype(f32)
    own[pl.ds(4, 4), :] = high
    own[pl.ds(8, 4), :] = moment[0] - high
    own[pl.ds(12, 4), :] = variance[0]
    pay[...] = own[...].astype(bf16)
    zbuf[z % 4, z // 4] = own[...].astype(bf16)

    pl.semaphore_wait(barrier, 22)

    span_far = [send(pay, zbuf.at[z % 4, z // 4], z_peers[k - 1]) for k in (8, 4, 12)]

    def tokens_z(i):
        lanes = pl.ds((i // 2) * QUARTER, QUARTER)
        return send(sources[i % 2].at[0, :, lanes], tok_one.at[i % 2, rows_one, lanes], partner)

    def rows_of(stream, y_of):
        if stream == "two":
            return pl.ds(pl.multiple_of(y_of * 16, 16), 16)
        z_of = zh if stream == "one" else 1 - zh
        return pl.ds(pl.multiple_of((y_of * 2 + z_of) * 16, 16), 16)

    y_up, y_down = (y + 1) % 4, (y + 3) % 4
    ways = {}

    def buffer(stream, i, y_of):
        lanes = pl.ds((i // 2) * QUARTER, QUARTER)
        tok = tok_two if stream == "two" else tok_one
        return tok.at[i % 2, rows_of(stream, y_of), lanes]

    def hand_on(stream, i, whole=False):
        lanes = pl.ds((i // 2) * QUARTER, QUARTER)
        block = buffer(stream, i, y)
        src = block
        if stream != "far":
            src = sources[i % 2].at[1 if stream == "two" else 0, :, lanes]
        copies = [send(src, block, at_y(y_up)), send(src, block, at_y(y_down))]
        if whole:
            copies.append(send(src, block, at_y((y + 2) % 4)))
        ways[stream, i] = copies

    def relay(stream, i):
        copies = ways[stream, i]
        if len(copies) == 3:
            return
        copies[i % 2].wait_recv()
        block = buffer(stream, i, (y_down, y_up)[i % 2])
        copies.append(send(block, block, at_y((y_up, y_down)[i % 2])))
        copies.pop(i % 2)

    def arrive(stream, i):
        for copy in ways[stream, i]:
            copy.wait_recv()

    across = [tokens_z(0), tokens_z(1)]
    for i in range(8):
        hand_on("one", i)
    for i in range(8):
        hand_on("two", i)
    for copy in span_far:
        copy.wait_recv()
    held = zbuf.at[z % 4]
    span_near = [
        send(held, held, at_z((z + 1) % 16)),
        send(held, held, at_z((z + 15) % 16)),
        send(held, held, at_z((z + 2 + 12 * (z % 2)) % 16)),
    ]
    across += [tokens_z(i) for i in range(2, 8)]

    for i in range(4):
        relay("one", i)

    def pass_on(i):
        across[i].wait_recv()
        hand_on("far", i, whole=i >= 6)
        if i == 0:
            for n in range(4, 8):
                relay("one", n)
        elif i <= 2:
            for n in range(4):
                relay("two", 4 * i - 4 + n)
        if i >= 1:
            relay("far", i - 1)

    later[0].wait()
    source = lax.broadcasted_iota(jnp.int32, (256, 512), 0)
    lane = lax.broadcasted_iota(jnp.int32, (256, 512), 1)
    segment = ((lane >> 4) & 1) * 128 + (lane & 7) * 16 + (lane >> 5)
    slots = jnp.broadcast_to(slot[...].reshape(1, 256).astype(f32), (16, 256)).astype(bf16)
    slot_row = dot_nn(slots, jnp.where(source == segment, 1.0, 0.0).astype(bf16))[0:1]
    at = lax.broadcasted_iota(jnp.int32, (512, 512), 0)
    lane = lax.broadcasted_iota(jnp.int32, (512, 512), 1)
    holds = ((at >> 6) & 3) * 64 + ((at >> 2) & 7) * 8 + (at >> 8) * 4 + (at & 3)
    same = (holds.astype(f32) == slot_row) & (((at >> 5) & 1) == ((lane >> 3) & 1))
    chosen[...] = jnp.where(same, 1.0, 0.0).astype(bf16)
    lane = lax.broadcasted_iota(jnp.int32, (256, 256), 1)
    segment = ((lane >> 3) & 1) * 128 + (lane & 7) * 16 + (lane >> 4)
    source = lax.broadcasted_iota(jnp.int32, (256, 256), 0)
    slot_row = dot_nn(slots, jnp.where(source == segment, 1.0, 0.0).astype(bf16))[0:1]
    at = source
    holds = ((at >> 5) & 3) * 64 + ((at >> 2) & 7) * 8 + (at >> 7) * 4 + (at & 3)
    chosen_p = jnp.where(holds.astype(f32) == slot_row, 1.0, 0.0).astype(bf16)
    to = lax.broadcasted_iota(jnp.int32, (256, 256), 0)
    frm = lax.broadcasted_iota(jnp.int32, (256, 256), 1)
    wanted = ((to >> 2) & 3) * 64 + ((to >> 4) & 3) * 16 + (to >> 6) * 4 + (to & 3)
    order = jnp.where(frm == wanted, 1.0, 0.0).astype(bf16)

    pass_on(0)
    pass_on(1)
    for copy in span_near:
        copy.wait_recv()
    ordered = dot_nn(order, zbuf[...].reshape(256, SEG)).astype(bf16)

    def span_rows(core_of, x_of):
        return pl.ds(pl.multiple_of((core_of * 4 + x_of) * 64, 64), 64)

    for kind in range(4):
        xs[kind] = ordered[kind * 64 : (kind + 1) * 64]
        gathered[kind, span_rows(c, x), :] = ordered[kind * 64 : (kind + 1) * 64]
    span_x = [send(xs, gathered.at[:, span_rows(c, x), :], p) for p in x_peers]
    span_core = [send(xs, gathered.at[:, span_rows(c, x), :], core)]
    pass_on(2)
    for k in (1, 3, 2):
        span_x[k - 1].wait_recv()
        held = gathered.at[:, span_rows(c, (x + 4 - k) % 4), :]
        span_core.append(send(held, held, core))
    pass_on(3)
    pass_on(4)
    pass_on(5)
    for copy in span_core:
        copy.wait_recv()

    spread = dot_tn(chosen[...], gathered[0])
    for cs in range(16):
        for p in range(2):
            lanes = slice(cs * SEG, (cs + 1) * SEG)
            weights[p, :, lanes] = spread[cs * 32 + p * 16 : cs * 32 + p * 16 + 16].astype(bf16)
    spread = dot_tn(chosen[...], gathered[1]) + dot_tn(chosen[...], gathered[2])
    for cs in range(16):
        for p in range(2):
            lanes = slice(cs * SEG, (cs + 1) * SEG)
            mom[p, :, lanes] = spread[cs * 32 + p * 16 : cs * 32 + p * 16 + 16]
    spread = jnp.sqrt(dot_tn(chosen[...], gathered[3])) + epsilon
    for cs in range(16):
        for p in range(2):
            lanes = slice(cs * SEG, (cs + 1) * SEG)
            den[p, :, lanes] = spread[cs * 32 + p * 16 : cs * 32 + p * 16 + 16]
    pass_on(6)
    pass_on(7)

    def factors(before, back):
        before = up_scale * before
        back = down_scale * back
        hidden = (before * jax.nn.sigmoid(before)).astype(bf16)
        slope = (back * silu_slope(before)).astype(bf16)
        return slope, hidden

    for i in range(8):
        arrive("one", i)
    for copy in later[1:]:
        copy.wait()
    sums = [0.0, 0.0]
    for q in range(4):
        lanes = slice(q * QUARTER, (q + 1) * QUARTER)
        for a in (0, 1):
            arrive("far", 2 * q + a)
            sums[a] = sums[a] + dot_nt(weights[a, :, lanes], tok_one[a, :, lanes])
    both = factors(*sums)
    for p in range(2):
        scale = (up_scale, down_scale)[p]
        for n in range(16):
            lanes = slice(n * SEG, (n + 1) * SEG)
            step_one = scale * dot_nn(both[p], tok_one[p, :, lanes])
            moved = beta_one * mom[p, :, lanes] + (1.0 - beta_one) * step_one
            mom[p, :, lanes] = moved
            weights[p, :, lanes] = (
                weights[p, :, lanes].astype(f32) - step_rate * moved / den[p, :, lanes]
            ).astype(bf16)

    for i in range(8):
        arrive("two", i)
    both = factors(dot_nt(weights[0], tok_two[0]), dot_nt(weights[1], tok_two[1]))
    for p in range(2):
        scale = (up_scale, down_scale)[p]
        for n in range(16):
            step_two = scale * dot_nn(both[p], tok_two[p, :, n * SEG : (n + 1) * SEG])
            rows_g[pl.ds(n * 32 + p * 16, 16), :] = step_two.astype(bf16)
    flat_g[...] = dot_nn(chosen[...], rows_g[...]).astype(bf16)

    def reduce_core(flat, rc, nz):
        rows = 16 * nz
        return send(flat.at[pl.ds(pl.multiple_of((1 - c) * rows, rows), rows), :], rc, core)

    def reduce_x(copy, flat, rc, sf, sb, rx, nz):
        rows, part = 16 * nz, 4 * nz
        copy.wait_recv()
        total = flat[pl.ds(pl.multiple_of(c * rows, rows), rows), :].astype(f32) + rc[...].astype(f32)
        sf[...] = total
        sb[...] = total.astype(bf16)
        return [
            send(sb.at[pl.ds(pl.multiple_of(((x + k) % 4) * part, part), part), :], rx.at[k - 1], x_peers[k - 1])
            for k in range(1, 4)
        ]

    def reduce_z(copies, sf, rx, ff, fb, rz, nz, peers, me):
        part = 4 * nz
        for copy in copies:
            copy.wait_recv()
        total = sf[pl.ds(pl.multiple_of(x * part, part), part), :]
        for k in range(3):
            total = total + rx[k].astype(f32)
        for i in range(nz):
            for t in range(4):
                ff[i, pl.ds(t * 4, 4), :] = total[i * 4 : i * 4 + 4, t * 128 : (t + 1) * 128]
        fb[...] = ff[...].astype(bf16)
        return [
            send(fb.at[(me + k) % nz], rz.at[k - 1], peers[k - 1]) for k in range(1, nz)
        ]

    def reduce_end(copies, ff, rz, nz, me):
        for copy in copies:
            copy.wait_recv()
        total = ff[me]
        for k in range(nz - 1):
            total = total + rz[k].astype(f32)
        return jnp.concatenate([total[t * 4 : t * 4 + 4] for t in range(4)], axis=1)

    step_g = reduce_core(flat_g, rc_g, 16)
    own_rows = pl.ds(pl.multiple_of(zh * 8, 8), 8)
    for p in range(2):
        shifted = mom[p, own_rows, :] + feedback[0, p].astype(f32)
        magnitude = jnp.sum(jnp.abs(shifted), axis=-1, keepdims=True) / D + 1e-06
        packed = magnitude * jnp.tanh(shifted / magnitude)
        feedback_out[0, p] = (shifted - packed).astype(bf16)
        for cs in range(16):
            rows_p[pl.ds(cs * 16 + p * 8, 8), :] = packed[:, cs * SEG : (cs + 1) * SEG]
    flat_p[...] = dot_nn(chosen_p, rows_p[...].astype(bf16)).astype(bf16)
    step_p = reduce_core(flat_p, rc_p, 8)
    step_g = reduce_x(step_g, flat_g, rc_g, sf_g, sb_g, rx_g, 16)
    step_p = reduce_x(step_p, flat_p, rc_p, sf_p, sb_p, rx_p, 8)
    step_g = reduce_z(step_g, sf_g, rx_g, ff_g, fb_g, rz_g, 16, z_peers, z)
    step_p = reduce_z(step_p, sf_p, rx_p, ff_p, fb_p, rz_p, 8, zl_peers, zl)
    mean_moment = reduce_end(step_p, ff_p, rz_p, 8, zl) / 64
    mean_grad = reduce_end(step_g, ff_g, rz_g, 16, z) / 64
    moment_new = beta_one * mean_moment + (1.0 - beta_one) * mean_grad
    moment_out[0] = moment_new
    owner_denominator = jnp.sqrt(variance[0]) + epsilon
    master_out[0] = master[0] - step_rate * (mean_moment + moment_new) / owner_denominator
    for copy in started:
        copy.wait_send()


def per_device(master, moment, variance, flat_slot, feedback, activations, output_grads):
    vmem = pl.BlockSpec(memory_space=pltpu.VMEM)
    hbm = pl.BlockSpec(memory_space=pl.ANY)

    def reduction(nz):
        return [
            pltpu.VMEM((32 * nz, SEG), bf16),
            pltpu.VMEM((16 * nz, SEG), bf16),
            pltpu.VMEM((16 * nz, SEG), f32),
            pltpu.VMEM((16 * nz, SEG), bf16),
            pltpu.VMEM((3, 4 * nz, SEG), bf16),
            pltpu.VMEM((nz, 16, 128), f32),
            pltpu.VMEM((nz, 16, 128), bf16),
            pltpu.VMEM((nz - 1, 16, 128), bf16),
        ]

    span = pltpu.VMEM(master.shape, f32)
    scratch = [
        span,
        span,
        span,
        pltpu.VMEM(flat_slot.shape, jnp.int32),
        pltpu.VMEM(feedback.shape, bf16),
        pltpu.VMEM((16, SEG), f32),
        pltpu.VMEM((16, SEG), bf16),
        pltpu.VMEM((4, 4, 16, SEG), bf16),
        pltpu.VMEM((4, 64, SEG), bf16),
        pltpu.VMEM((4, 512, SEG), bf16),
        pltpu.VMEM((512, 512), bf16),
        pltpu.VMEM((2, 16, D), bf16),
        pltpu.VMEM((2, 16, D), f32),
        pltpu.VMEM((2, 16, D), f32),
        pltpu.VMEM((2, 128, D), bf16),
        pltpu.VMEM((2, 64, D), bf16),
        pltpu.VMEM((256, SEG), f32),
        *reduction(8),
        pltpu.VMEM((512, SEG), bf16),
        *reduction(16),
        pltpu.SemaphoreType.DMA((N_COPIES,)),
        pltpu.SemaphoreType.DMA((N_COPIES,)),
        pltpu.SemaphoreType.DMA((9,)),
    ]
    return pl.pallas_call(
        kernel,
        out_shape=(
            jax.ShapeDtypeStruct(master.shape, f32),
            jax.ShapeDtypeStruct(moment.shape, f32),
            jax.ShapeDtypeStruct(feedback.shape, bf16),
        ),
        in_specs=[hbm] * 7,
        out_specs=(vmem,) * 3,
        scratch_shapes=scratch,
        compiler_params=pltpu.CompilerParams(collective_id=0, has_side_effects=True),
        name="window",
    )(master, moment, variance, flat_slot, feedback, activations, output_grads)


def solution(mesh):
    in_specs = (
        P("mp", "dp", None),
        P("mp", "dp", None),
        P("mp", "dp", None),
        P(),
        P("dp", None, "mp", None),
        P(None, ("dp", "mp"), None),
        P(None, ("dp", "mp"), None),
    )
    out_specs = (P("mp", "dp", None), P("mp", "dp", None), P("dp", None, "mp", None))
    return jax.shard_map(
        per_device, mesh=mesh, in_specs=in_specs, out_specs=out_specs, check_vma=False
    )
```
